32 devices in a mesh: fsdp: 4 (over y, x), ctx: 2 (over core), tp: 4 (over z).
Axes of the slice: x: 2, y: 2, z: 4, core: 2. Of those that a mesh axis runs over, the one named last changes fastest.
Arguments:
- tokens: bfloat16 [4, 2048, 2048], P('fsdp', 'ctx'), may hold values from -6 to 6
- cotangent: bfloat16 [4, 2048, 2048], P('fsdp', 'ctx'), may hold values from -6 to 6
- piece_starts: int32 [4, 3], P('fsdp'), may hold values from 0 to 1790, as said below
- attn_gain: bfloat16 [2048], P(('fsdp', 'ctx')), may hold values from 0.5 to 1.5
- query_down: bfloat16 [2048, 1024], P(('fsdp', 'ctx')), may hold values from -0.125 to 0.125
- query_gain: bfloat16 [1024], P(('fsdp', 'ctx')), may hold values from 0.5 to 1.5
- query_up: bfloat16 [1024, 4096], P(('fsdp', 'ctx'), 'tp'), may hold values from -0.1875 to 0.1875
- key_proj: bfloat16 [2048, 256], P(('fsdp', 'ctx')), may hold values from -0.125 to 0.125
- value_proj: bfloat16 [2048, 256], P(('fsdp', 'ctx')), may hold values from -0.125 to 0.125
- out_proj: bfloat16 [4096, 2048], P('tp', ('fsdp', 'ctx')), may hold values from -1 to 1
- ffn_gain: bfloat16 [2048], P(('fsdp', 'ctx')), may hold values from 0.5 to 1.5
- gate_proj: bfloat16 [2048, 5632], P(('fsdp', 'ctx'), 'tp'), may hold values from -0.125 to 0.125
- up_proj: bfloat16 [2048, 5632], P(('fsdp', 'ctx'), 'tp'), may hold values from -0.125 to 0.125
- down_proj: bfloat16 [5632, 2048], P('tp', ('fsdp', 'ctx')), may hold values from -0.078125 to 0.078125
Outputs:
- layer_out: bfloat16 [4, 2048, 2048], P('fsdp', 'ctx')
- tokens_grad: bfloat16 [4, 2048, 2048], P('fsdp', 'ctx')
- attn_gain_grad: float32 [2048], P(('fsdp', 'ctx'))
- query_down_grad: float32 [2048, 1024], P(('fsdp', 'ctx'))
- query_gain_grad: float32 [1024], P(('fsdp', 'ctx'))
- query_up_grad: float32 [1024, 4096], P(('fsdp', 'ctx'), 'tp')
- key_proj_grad: float32 [2048, 256], P(('fsdp', 'ctx'))
- value_proj_grad: float32 [2048, 256], P(('fsdp', 'ctx'))
- out_proj_grad: float32 [4096, 2048], P('tp', ('fsdp', 'ctx'))
- ffn_gain_grad: float32 [2048], P(('fsdp', 'ctx'))
- gate_proj_grad: float32 [2048, 5632], P(('fsdp', 'ctx'), 'tp')
- up_proj_grad: float32 [2048, 5632], P(('fsdp', 'ctx'), 'tp')
- down_proj_grad: float32 [5632, 2048], P('tp', ('fsdp', 'ctx'))
The draws below stay inside these ranges and needn't reach their ends.
Inputs may be any that keep to these rules, and one draw needn't show every extreme that they name: `piece_starts`: in each sequence piece k starts at or after k * (682) and ends by (k + 1) * 682, so pieces never intersect and starts rise.
All inputs are finite; a program needn't handle non-finite values.
Results may differ from the reference program's by a relative error of at most 0.024.
Values may be sent and summed in bfloat16 or wider, within the bound.
No kernel may reach another device: no remote copies, remote signals or barrier semaphores. Data moves between devices by JAX's collectives and lax.ppermute only.
A program may use at most 256 MiB of HBM per device.

```python
import jax
import jax.numpy as jnp
from jax import lax

D = 2048
QR = 1024
HEADS = 16
HD = 256
FF = 5632
LEN = 2048
PIECE = 256
PIECES = 3
SEQS = 4


def draw_piece_starts(key, part):
    region = LEN // PIECES
    widest = region - PIECE
    offsets = jax.random.randint(key, (SEQS, PIECES), 0, widest + 1).astype(jnp.int32)
    rows = jnp.arange(SEQS).astype(jnp.int32)[:, None]
    cols = jnp.arange(PIECES).astype(jnp.int32)[None, :]
    offsets = jnp.where((rows == 0) & (cols == 0), 0, offsets)
    offsets = jnp.where((rows == 0) & (cols == PIECES - 1), widest, offsets)
    return (cols * region + offsets).astype(jnp.int32)


def steps_of(rng, dims, cuts, least, top_value):
    def one(axis_at, shards_of):
        heights = jax.random.uniform(jax.random.fold_in(jax.random.fold_in(rng, 6), axis_at), (shards_of,), jnp.float32, least / len(cuts), top_value / len(cuts))
        return jnp.repeat(jnp.exp(heights), dims[axis_at] // shards_of).reshape((-1,) + (1,) * (len(dims) - axis_at - 1))

    level = one(*cuts[0])
    for cut in cuts[1:]:
        level = level * one(*cut)
    return level


def bell_draw(key, extent, deviation, limit, cuts=(), dtype=jnp.bfloat16):
    drawn = jax.random.normal(key, extent, jnp.float32) * deviation
    if len(cuts) > 0:
        drawn = steps_of(key, extent, cuts, -0.22, 0.18) * drawn
    return jnp.clip(drawn, min=-limit, max=limit).astype(dtype)


def setup_inputs(seed: int = 0) -> dict:
    key_list = jax.random.split(jax.random.key(seed), 15)
    return {
        "tokens": bell_draw(key_list[0], (SEQS, LEN, D), 1.0, 6.0, ((0, 4), (1, 2))),
        "cotangent": bell_draw(key_list[1], (SEQS, LEN, D), 1.0, 6.0, ((0, 4), (1, 2))),
        "piece_starts": draw_piece_starts(jax.random.fold_in(key_list[14], 71), 0),
        "attn_gain": jnp.clip(1.0 + 0.1 * jax.random.normal(key_list[3], (D,), jnp.float32), 0.5, 1.5).astype(jnp.bfloat16),
        "query_down": bell_draw(key_list[4], (D, QR), D ** -0.5, 0.125, ((0, 8),)),
        "query_gain": jnp.clip(1.0 + 0.1 * jax.random.normal(key_list[5], (QR,), jnp.float32), 0.5, 1.5).astype(jnp.bfloat16),
        "query_up": bell_draw(key_list[6], (QR, HEADS * HD), QR ** -0.5, 0.1875, ((0, 8), (1, 4))),
        "key_proj": bell_draw(key_list[7], (D, HD), D ** -0.5, 0.125, ((0, 8),)),
        "value_proj": bell_draw(key_list[8], (D, HD), D ** -0.5, 0.125, ((0, 8),)),
        "out_proj": bell_draw(key_list[9], (HEADS * HD, D), (HEADS * HD // 128) ** -0.5, 1.0, ((0, 4), (1, 8))),
        "ffn_gain": jnp.clip(1.0 + 0.1 * jax.random.normal(key_list[10], (D,), jnp.float32), 0.5, 1.5).astype(jnp.bfloat16),
        "gate_proj": bell_draw(key_list[11], (D, FF), D ** -0.5, 0.125, ((0, 8), (1, 4))),
        "up_proj": bell_draw(key_list[12], (D, FF), D ** -0.5, 0.125, ((0, 8), (1, 4))),
        "down_proj": bell_draw(key_list[13], (FF, D), FF ** -0.5, 0.078125, ((0, 4), (1, 8))),
    }


norm_eps = 1e-05
masked_score = -1e+30
highest = lax.Precision.HIGHEST

@jax.custom_vjp
def low(v):
    return lax.optimization_barrier(v.astype(jnp.bfloat16)).astype(jnp.float32)

@jax.custom_vjp
def low_back(v):
    return v

def low_keep(v):
    return (low(v), None)

def low_pass(kept, grad):
    return (grad,)

def back_keep(v):
    return (v, None)

def back_low(kept, grad):
    return (low(grad),)
low.defvjp(low_keep, low_pass)
low_back.defvjp(back_keep, back_low)

def rope_tables(positions, width):
    half_width = width // 2
    freqs = jnp.exp(-jnp.log(10000.0) * jnp.arange(half_width).astype(jnp.float32) * 2.0 / width)
    angles = positions.astype(jnp.float32)[:, None] * freqs[None, :]
    return (jnp.cos(angles), jnp.sin(angles))

def rotate(vectors, cosine, sine):
    half_width = vectors.shape[-1] // 2
    first, second = (vectors[..., :half_width], vectors[..., half_width:])
    return jnp.concatenate([first * cosine - second * sine, second * cosine + first * sine], axis=-1)

def piece_ids(positions, starts):
    inside = (positions[:, None] >= starts[None, :]) & (positions[:, None] < starts[None, :] + PIECE)
    numbers = jnp.arange(1, starts.shape[0] + 1).astype(jnp.int32)
    return (lax.optimization_barrier(jnp.sum(jnp.where(inside, numbers[None, :], 0), axis=1)) - 1).astype(jnp.int32)

def rms_scale(values, norm_weight):
    return values * lax.rsqrt(lax.optimization_barrier(jnp.mean(values * values, axis=-1, keepdims=True)) + norm_eps) * norm_weight

def one_sequence(seq_rows, starts, weights):
    attn_gain, query_down, query_gain, query_up, key_proj, value_proj, out_proj, ffn_gain, gate_proj, up_proj, down_proj = weights
    length = seq_rows.shape[0]
    positions = jnp.arange(length).astype(jnp.int32)
    cosine, sine = rope_tables(positions, HD)
    normed_one = low(rms_scale(seq_rows, attn_gain))
    latent = low_back(jnp.dot(normed_one, query_down, precision=highest))
    latent_normed = low(rms_scale(latent, query_gain))
    query_lin = low_back(jnp.dot(latent_normed, query_up, precision=highest)).reshape(length, HEADS, HD)
    queries = low(rotate(query_lin, cosine[:, None, :], sine[:, None, :]))
    key_lin = low_back(jnp.dot(normed_one, key_proj, precision=highest))
    key_rows = low(rotate(key_lin, cosine, sine))
    values = low(low_back(jnp.dot(normed_one, value_proj, precision=highest)))
    labels = piece_ids(positions, starts)
    block_rows = min(512, length)
    score_scale = HD ** (-0.5)

    def attend(block_index):
        row_start = block_index * block_rows
        query_block = lax.dynamic_slice_in_dim(queries, row_start, block_rows, 0)
        query_pos = row_start + jnp.arange(block_rows).astype(jnp.int32)
        query_lab = lax.dynamic_slice_in_dim(labels, row_start, block_rows, 0)
        scores = low_back(jnp.einsum('qhd,kd->hqk', query_block, key_rows, precision=highest) * score_scale)
        allowed = (positions[None, :] <= query_pos[:, None]) | (query_lab[:, None] == labels[None, :]) & (query_lab[:, None] >= 0)
        scores = jnp.where(allowed[None], scores, masked_score)
        top_score = lax.optimization_barrier(jnp.max(scores, axis=-1, keepdims=True))
        expo = jnp.exp(scores - top_score)
        attn_probs = low(expo / lax.optimization_barrier(jnp.sum(expo, axis=-1, keepdims=True)))
        return jnp.einsum('hqk,kd->qhd', attn_probs, values, precision=highest)
    blocks_out = lax.map(jax.checkpoint(attend), jnp.arange(length // block_rows))
    attended = low(low_back(blocks_out.reshape(length, HEADS * HD)))
    attn_branch = low_back(jnp.dot(attended, out_proj, precision=highest))
    hidden_state = seq_rows + attn_branch
    normed_two = low(rms_scale(hidden_state, ffn_gain))
    gate_vals = low_back(jnp.dot(normed_two, gate_proj, precision=highest))
    up_vals = low_back(jnp.dot(normed_two, up_proj, precision=highest))
    activ = low(gate_vals * jax.nn.sigmoid(gate_vals) * up_vals)
    return hidden_state + jnp.dot(activ, down_proj, precision=highest)

def reference(tokens, cotangent, piece_starts, attn_gain, query_down, query_gain, query_up, key_proj, value_proj, out_proj, ffn_gain, gate_proj, up_proj, down_proj):
    floats = tuple((w.astype(jnp.float32) for w in (attn_gain, query_down, query_gain, query_up, key_proj, value_proj, out_proj, ffn_gain, gate_proj, up_proj, down_proj)))
    token_rows = tokens.astype(jnp.float32)

    def forward(all_rows, *weights):

        def one_step(paired):
            return one_sequence(paired[0], paired[1], weights)
        return lax.map(jax.checkpoint(one_step), (all_rows, piece_starts))
    layer_out, pullback = jax.vjp(forward, token_rows, *floats)
    grads = pullback(cotangent.astype(jnp.float32))
    return (layer_out.astype(jnp.bfloat16), grads[0].astype(jnp.bfloat16), grads[1], grads[2], grads[3], grads[4], grads[5], grads[6], grads[7], grads[8], grads[9], grads[10], grads[11])
```

```python
import functools

import jax
import jax.numpy as jnp
from jax import lax
from jax.experimental import pallas as pl
from jax.experimental.pallas import tpu as pltpu
from jax.sharding import PartitionSpec as P

PIECE = 256

norm_eps = 1e-05
masked_score = -1e30
BQ = 256
BK = 512
f32 = jnp.float32
bf16 = jnp.bfloat16
WEIGHT_AXES = ("fsdp", "ctx")


def rope_tables(positions, width):
    half_width = width // 2
    freqs = jnp.exp(-jnp.log(10000.0) * jnp.arange(half_width).astype(f32) * 2.0 / width)
    angles = positions.astype(f32)[:, None] * freqs[None, :]
    return (jnp.cos(angles), jnp.sin(angles))


def nn(a, b):
    return jnp.dot(a, b, preferred_element_type=f32)


def tn(a, b):
    return lax.dot_general(a, b, (((0,), (0,)), ((), ())), preferred_element_type=f32)


def nt(a, b):
    return lax.dot_general(a, b, (((1,), (1,)), ((), ())), preferred_element_type=f32)


def halves(a, axis=0):
    return jnp.split(a, 2, axis=axis)


def exchanged():
    return lax.axis_size("fsdp") == 4 and lax.axis_size("ctx") == 2


def over_x(a):
    return lax.ppermute(a, "fsdp", [(i, i ^ 1) for i in range(4)])


def over_y(a):
    return lax.ppermute(a, "fsdp", [(i, i ^ 2) for i in range(4)])


def over_ctx(a):
    return lax.ppermute(a, "ctx", [(0, 1), (1, 0)])


def block_order():
    shards = lax.axis_size("fsdp") * lax.axis_size("ctx")
    if not exchanged():
        return jnp.arange(8, dtype=jnp.int32)
    f = lax.axis_index("fsdp")
    c = lax.axis_index("ctx")
    j = jnp.arange(shards, dtype=jnp.int32)
    return (((j % 4) ^ f) * 2 + ((j // 4) ^ c)).astype(jnp.int32)


def place_order():
    n = jnp.arange(8, dtype=jnp.int32)
    if not exchanged():
        return n
    f = lax.axis_index("fsdp")
    c = lax.axis_index("ctx")
    return (((n // 2) ^ f) + ((n % 2) ^ c) * 4).astype(jnp.int32)


def gather(w, axis):
    if not exchanged():
        return halves(lax.all_gather(w, WEIGHT_AXES, axis=axis, tiled=True), axis)
    a, b = halves(w)
    ax, bx, ay, by = over_x(a), over_x(b), over_y(a), over_y(b)
    ad, bd = over_x(ay), over_y(bx)
    if axis == 0:
        mine = jnp.concatenate([w, ax, bx, ay, by, ad, bd], axis=0)
    else:
        mine = jnp.concatenate(
            [
                jnp.concatenate([a, ax, ay, ad], axis=1),
                jnp.concatenate([b, bx, by, bd], axis=1),
            ],
            axis=0,
        )
    return mine, over_ctx(mine)


def scatter(make_mine, make_other, axis):
    if not exchanged():
        whole = jnp.concatenate([make_mine().astype(bf16), make_other().astype(bf16)], axis=axis)
        return lax.psum_scatter(whole, WEIGHT_AXES, scatter_dimension=axis, tiled=True).astype(f32)
    got = over_ctx(make_other().astype(bf16))
    both = (make_mine() + got.astype(f32)).astype(bf16)
    own, x, y, d = jnp.split(both, 4, axis=axis)
    own_a, own_b = halves(own)
    x_a, x_b = halves(x)
    y_a, y_b = halves(y)
    d_a, d_b = halves(d)
    add = lambda p, q: p.astype(f32) + q.astype(f32)
    y_a = add(y_a, over_x(d_a)).astype(bf16)
    x_b = add(x_b, over_y(d_b)).astype(bf16)
    own_a = add(own_a, over_x(x_a))
    own_b = add(own_b, over_y(y_b))
    own_a = add(own_a, over_y(y_a))
    own_b = add(own_b, over_x(x_b))
    return jnp.concatenate([own_a, own_b], axis=0)


def take_kernel(order, a_ref, b_ref, left_ref, right_ref):
    left_ref[...] = a_ref[...]
    right_ref[...] = b_ref[...]


def take_blocks(a, order):
    rows, width = a.shape
    block = width // 8
    spec = lambda index: pl.BlockSpec((rows, block), index)
    return pl.pallas_call(
        take_kernel,
        out_shape=[jax.ShapeDtypeStruct((rows, width // 2), a.dtype)] * 2,
        grid_spec=pltpu.PrefetchScalarGridSpec(
            num_scalar_prefetch=1,
            grid=(4,),
            in_specs=[spec(lambda j, o: (0, o[j])), spec(lambda j, o: (0, o[4 + j]))],
            out_specs=[spec(lambda j, o: (0, j))] * 2,
        ),
        name="take_blocks",
    )(order, a, a)


def put_kernel(order, a_ref, b_ref, out_ref):
    @pl.when(pl.program_id(0) < 4)
    def _():
        out_ref[...] = a_ref[...]

    @pl.when(pl.program_id(0) >= 4)
    def _():
        out_ref[...] = b_ref[...]


def put_blocks(left, right, order):
    rows, half = left.shape
    block = half // 4
    spec = lambda index: pl.BlockSpec((rows, block), index)
    return pl.pallas_call(
        put_kernel,
        out_shape=jax.ShapeDtypeStruct((rows, 2 * half), left.dtype),
        grid_spec=pltpu.PrefetchScalarGridSpec(
            num_scalar_prefetch=1,
            grid=(8,),
            in_specs=[
                spec(lambda j, o: (0, jnp.minimum(j, 3))),
                spec(lambda j, o: (0, jnp.maximum(j - 4, 0))),
            ],
            out_specs=spec(lambda j, o: (0, o[j])),
        ),
        name="put_blocks",
    )(order, left, right)


def put_rows(left, right, order):
    half, width = left.shape
    block = half // 4
    spec = lambda index: pl.BlockSpec((block, width), index)
    return pl.pallas_call(
        put_kernel,
        out_shape=jax.ShapeDtypeStruct((2 * half, width), left.dtype),
        grid_spec=pltpu.PrefetchScalarGridSpec(
            num_scalar_prefetch=1,
            grid=(8,),
            in_specs=[
                spec(lambda j, o: (jnp.minimum(j, 3), 0)),
                spec(lambda j, o: (jnp.maximum(j - 4, 0), 0)),
            ],
            out_specs=spec(lambda j, o: (o[j], 0)),
        ),
        name="put_rows",
    )(order, left, right)


def label_of(position, info):
    label = jnp.full(position.shape, -1, jnp.int32)
    for k in range(info.shape[0] - 2):
        start = info[2 + k]
        label = jnp.where((position >= start) & (position < start + PIECE), k, label)
    return label


def visible(info, row0, key0, heads):
    key_pos = key0 + lax.broadcasted_iota(jnp.int32, (BK, 128), 0)
    query_pos = row0 + lax.broadcasted_iota(jnp.int32, (8, BQ), 1)
    key_lab = label_of(key_pos, info)[:, :1]
    query_lab = label_of(query_pos, info)[:1, :]
    seen = (key_pos[:, :1] <= query_pos[:1, :]) | ((key_lab == query_lab) & (key_lab >= 0))
    bias = jnp.where(seen, 0.0, masked_score).astype(f32)
    return jnp.concatenate([bias] * heads, axis=1)


def key_blocks(row0, length):
    full = row0 // BK
    reach = jnp.minimum(row0 + BQ + PIECE - 1, length)
    return full, (reach + BK - 1) // BK


def keys_ds(info, half, which):
    start = info[which] * half
    return pl.ds(pl.multiple_of(start, half), half)


def attend_kernel(
    info, qn, up, k_own, v_own, k_oth, v_oth, cos, sin,
    q_out, o_out, lse_out,
    keys, values_t, qs, acc, top, total,
):
    i = pl.program_id(0)
    half, head = k_own.shape
    heads = q_out.shape[1] // head
    length = 2 * half
    hh = head // 2

    @pl.when(i == 0)
    def _():
        own, oth = keys_ds(info, half, 0), keys_ds(info, half, 1)
        keys[own, :] = k_own[...]
        keys[oth, :] = k_oth[...]
        values_t[:, own] = v_own[...].T
        values_t[:, oth] = v_oth[...].T

    row0 = info[0] * half + i * BQ
    scale = head ** (-0.5)
    for h in range(heads):
        lin = nn(qn[...], up[:, h * head : (h + 1) * head])
        a, b = lin[:, :hh], lin[:, hh:]
        c, s = cos[...], sin[...]
        q_h = jnp.concatenate([a * c - b * s, b * c + a * s], axis=1)
        q_h = (q_h * scale).astype(bf16)
        q_out[:, h * head : (h + 1) * head] = q_h
        qs[h * BQ : (h + 1) * BQ, :] = q_h

    top[...] = jnp.full(top.shape, -jnp.inf, f32)
    total[...] = jnp.zeros(total.shape, f32)
    acc[...] = jnp.zeros(acc.shape, f32)

    def step(kb, masked):
        key0 = pl.multiple_of(kb * BK, BK)
        s = nt(keys[pl.ds(key0, BK), :], qs[...])
        if masked:
            s = s + visible(info, row0, key0, heads)
        old = top[...]
        new = jnp.maximum(old, jnp.max(s, axis=0, keepdims=True))
        p = jnp.exp(s - new)
        alpha = jnp.exp(old - new)
        total[...] = total[...] * alpha + jnp.sum(p, axis=0, keepdims=True)
        acc[...] = acc[...] * alpha + nn(values_t[:, pl.ds(key0, BK)], p.astype(bf16))
        top[...] = new

    full, last = key_blocks(row0, length)
    pl.loop(0, full)(lambda kb: step(kb, False))
    pl.loop(full, last)(lambda kb: step(kb, True))
    o_t = acc[...] / total[...]
    for h in range(heads):
        o_out[:, h * head : (h + 1) * head] = o_t[:, h * BQ : (h + 1) * BQ].T.astype(bf16)
    lse_out[0] = top[...] + jnp.log(total[...])


def attend(info, qn, up, k_own, v_own, k_oth, v_oth, cos, sin):
    rows, rank = qn.shape
    half, head = k_own.shape
    width = up.shape[1]
    heads = width // head
    blocks = rows // BQ
    row = lambda w: pl.BlockSpec((BQ, w), lambda i, o: (i, 0))
    whole = lambda a: pl.BlockSpec(a.shape, lambda i, o: (0, 0))
    return pl.pallas_call(
        attend_kernel,
        out_shape=[
            jax.ShapeDtypeStruct((rows, width), bf16),
            jax.ShapeDtypeStruct((rows, width), bf16),
            jax.ShapeDtypeStruct((blocks, 1, heads * BQ), f32),
        ],
        grid_spec=pltpu.PrefetchScalarGridSpec(
            num_scalar_prefetch=1,
            grid=(blocks,),
            in_specs=[row(rank), whole(up), whole(k_own), whole(v_own), whole(k_oth), whole(v_oth), row(head // 2), row(head // 2)],
            out_specs=[row(width), row(width), pl.BlockSpec((1, 1, heads * BQ), lambda i, o: (i, 0, 0))],
            scratch_shapes=[
                pltpu.VMEM((2 * half, head), bf16),
                pltpu.VMEM((head, 2 * half), bf16),
                pltpu.VMEM((heads * BQ, head), bf16),
                pltpu.VMEM((head, heads * BQ), f32),
                pltpu.VMEM((1, heads * BQ), f32),
                pltpu.VMEM((1, heads * BQ), f32),
            ],
        ),
        compiler_params=pltpu.CompilerParams(vmem_limit_bytes=48 << 20),
        cost_estimate=pl.CostEstimate(
            flops=2 * rows * rank * width + 4 * rows * width * half * 2,
            bytes_accessed=16 << 20,
            transcendentals=rows * heads * 2 * half,
        ),
        name="attend",
    )(info, qn, up, k_own, v_own, k_oth, v_oth, cos, sin)


def attend_back_kernel(
    info, q, o, d_o, lse, k_own, v_own, k_oth, v_oth, cos, sin,
    dq_out, own_out, oth_out,
    keys, keys_t, values, qs, dos, dq_t, dk, dv,
):
    i = pl.program_id(0)
    half, head = k_own.shape
    heads = q.shape[1] // head
    length = 2 * half
    hh = head // 2
    own, oth = keys_ds(info, half, 0), keys_ds(info, half, 1)

    @pl.when(i == 0)
    def _():
        keys[own, :] = k_own[...]
        keys[oth, :] = k_oth[...]
        keys_t[:, own] = k_own[...].T
        keys_t[:, oth] = k_oth[...].T
        values[own, :] = v_own[...]
        values[oth, :] = v_oth[...]
        dk[...] = jnp.zeros(dk.shape, f32)
        dv[...] = jnp.zeros(dv.shape, f32)

    row0 = info[0] * half + i * BQ
    deltas = []
    for h in range(heads):
        cols = slice(h * head, (h + 1) * head)
        rows = slice(h * BQ, (h + 1) * BQ)
        qs[rows, :] = q[:, cols]
        dos[rows, :] = d_o[:, cols]
        product = d_o[:, cols].astype(f32) * o[:, cols].astype(f32)
        deltas.append(jnp.sum(product.T, axis=0, keepdims=True))
    delta = jnp.concatenate(deltas, axis=1)
    log_total = lse[0]
    dq_t[...] = jnp.zeros(dq_t.shape, f32)

    def step(kb, masked):
        key0 = pl.multiple_of(kb * BK, BK)
        at = pl.ds(key0, BK)
        s = nt(keys[at, :], qs[...])
        if masked:
            s = s + visible(info, row0, key0, heads)
        p = jnp.exp(s - log_total)
        dp = nt(values[at, :], dos[...])
        ds = (p * (dp - delta)).astype(bf16)
        dv[at, :] += nn(p.astype(bf16), dos[...])
        dk[at, :] += nn(ds, qs[...])
        dq_t[...] += nn(keys_t[:, at], ds)

    full, last = key_blocks(row0, length)
    pl.loop(0, full)(lambda kb: step(kb, False))
    pl.loop(full, last)(lambda kb: step(kb, True))
    scale = head ** (-0.5)
    c, s = cos[...], sin[...]
    for h in range(heads):
        g = dq_t[:, h * BQ : (h + 1) * BQ].T * scale
        a, b = g[:, :hh], g[:, hh:]
        back = jnp.concatenate([a * c + b * s, b * c - a * s], axis=1)
        dq_out[:, h * head : (h + 1) * head] = back.astype(bf16)

    @pl.when(i == pl.num_programs(0) - 1)
    def _():
        own_out[:, :head] = dk[own, :].astype(bf16)
        own_out[:, head:] = dv[own, :].astype(bf16)
        oth_out[:, :head] = dk[oth, :].astype(bf16)
        oth_out[:, head:] = dv[oth, :].astype(bf16)


def attend_back(info, q, o, d_o, lse, k_own, v_own, k_oth, v_oth, cos, sin):
    rows, width = q.shape
    half, head = k_own.shape
    heads = width // head
    blocks = rows // BQ
    row = lambda w: pl.BlockSpec((BQ, w), lambda i, o: (i, 0))
    whole = lambda a: pl.BlockSpec(a.shape, lambda i, o: (0, 0))
    kv_out = jax.ShapeDtypeStruct((half, 2 * head), bf16)
    return pl.pallas_call(
        attend_back_kernel,
        out_shape=[jax.ShapeDtypeStruct((rows, width), bf16), kv_out, kv_out],
        grid_spec=pltpu.PrefetchScalarGridSpec(
            num_scalar_prefetch=1,
            grid=(blocks,),
            in_specs=[row(width), row(width), row(width), pl.BlockSpec((1, 1, heads * BQ), lambda i, o: (i, 0, 0)), whole(k_own), whole(v_own), whole(k_oth), whole(v_oth), row(head // 2), row(head // 2)],
            out_specs=[row(width), whole(kv_out), whole(kv_out)],
            scratch_shapes=[
                pltpu.VMEM((2 * half, head), bf16),
                pltpu.VMEM((head, 2 * half), bf16),
                pltpu.VMEM((2 * half, head), bf16),
                pltpu.VMEM((heads * BQ, head), bf16),
                pltpu.VMEM((heads * BQ, head), bf16),
                pltpu.VMEM((head, heads * BQ), f32),
                pltpu.VMEM((2 * half, head), f32),
                pltpu.VMEM((2 * half, head), f32),
            ],
        ),
        compiler_params=pltpu.CompilerParams(vmem_limit_bytes=56 << 20),
        cost_estimate=pl.CostEstimate(
            flops=10 * rows * width * half * 2,
            bytes_accessed=16 << 20,
            transcendentals=rows * heads * 2 * half,
        ),
        name="attend_back",
    )(info, q, o, d_o, lse, k_own, v_own, k_oth, v_oth, cos, sin)


def mean_of(pair, width):
    return sum(jnp.sum(a, axis=-1, keepdims=True) for a in pair) / width


def sum_tp(*arrays):
    return lax.psum(tuple(a.astype(bf16) for a in arrays), "tp")


def norm_back(pair, inverse, gains, upstream, width):
    weighted = [u * g for u, g in zip(upstream, gains)]
    grads = [jnp.sum(u * v * inverse, axis=0) for u, v in zip(upstream, pair)]
    middle = mean_of([w * v for w, v in zip(weighted, pair)], width)
    cube = inverse * inverse * inverse
    return [inverse * w - v * cube * middle for w, v in zip(weighted, pair)], grads


def shards(
    tokens,
    cotangent,
    piece_starts,
    attn_gain,
    query_down,
    query_gain,
    query_up,
    key_proj,
    value_proj,
    out_proj,
    ffn_gain,
    gate_proj,
    up_proj,
    down_proj,
):
    _, half_len, width = tokens.shape
    rank = query_down.shape[1]
    head = key_proj.shape[1]
    ctx = lax.axis_index("ctx").astype(jnp.int32)
    order = block_order()
    info = jnp.concatenate([jnp.stack([ctx, 1 - ctx]), piece_starts[0].astype(jnp.int32)])

    n_gain, n_rank = attn_gain.shape[0], query_gain.shape[0]
    first_l, first_r = gather(jnp.concatenate([query_down, key_proj, value_proj], axis=1), 0)
    gains = jnp.concatenate([attn_gain, ffn_gain, query_gain]).reshape(1, -1)
    gains = jnp.concatenate([gains, gains], axis=0)
    gains_l, gains_r = gather(gains, 1)
    up_l, up_r = gather(query_up, 0)
    out_l, out_r = gather(out_proj, 1)
    gu_l, gu_r = gather(jnp.concatenate([gate_proj, up_proj], axis=1), 0)
    down_l, down_r = gather(down_proj, 1)

    def gain_of(part, lo, n):
        return part[0].reshape(-1, 2 * n_gain + n_rank)[:, lo : lo + n].reshape(1, -1).astype(f32)

    attn_g = [gain_of(p, 0, n_gain) for p in (gains_l, gains_r)]
    ffn_g = [gain_of(p, n_gain, n_gain) for p in (gains_l, gains_r)]
    query_g = jnp.concatenate(
        [gain_of(p, 2 * n_gain, n_rank) for p in (gains_l, gains_r)], axis=1
    ).reshape(8, -1)
    query_g = query_g[place_order()].reshape(1, rank)
    query_up_full = put_rows(up_l, up_r, order)

    positions = ctx * half_len + jnp.arange(half_len)
    cosine, sine = rope_tables(positions, head)

    rows_l, rows_r = take_blocks(tokens[0], order)
    x = [rows_l.astype(f32), rows_r.astype(f32)]
    inverse_one = lax.rsqrt(mean_of([a * a for a in x], width) + norm_eps)
    xn1 = [(a * inverse_one * g).astype(bf16) for a, g in zip(x, attn_g)]
    first = nn(xn1[0], first_l) + nn(xn1[1], first_r)
    latent = first[:, :rank]
    inverse_latent = lax.rsqrt(jnp.mean(latent * latent, axis=-1, keepdims=True) + norm_eps)
    qn = (latent * inverse_latent * query_g).astype(bf16)

    def rotate(u, c, s):
        a, b = u[:, : head // 2], u[:, head // 2 :]
        return jnp.concatenate([a * c - b * s, b * c + a * s], axis=1)

    k_own = rotate(first[:, rank : rank + head], cosine, sine).astype(bf16)
    v_own = first[:, rank + head :].astype(bf16)
    k_oth, v_oth = over_ctx(k_own), over_ctx(v_own)
    queries, attended, log_totals = attend(
        info, qn, query_up_full, k_own, v_own, k_oth, v_oth, cosine, sine
    )

    mixed = sum_tp(nn(attended, out_l), nn(attended, out_r))
    hidden = [a + m.astype(f32) for a, m in zip(x, mixed)]
    inverse_two = lax.rsqrt(mean_of([a * a for a in hidden], width) + norm_eps)
    xn2 = [(a * inverse_two * g).astype(bf16) for a, g in zip(hidden, ffn_g)]
    gu = nn(xn2[0], gu_l) + nn(xn2[1], gu_r)
    units = gu.shape[1] // 2
    gate, up = gu[:, :units], gu[:, units:]
    sigma = jax.nn.sigmoid(gate)
    silu = gate * sigma
    activ = (silu * up).astype(bf16)

    dy = take_blocks(cotangent[0], order)
    d_activ = nt(dy[0], down_l) + nt(dy[1], down_r)
    d_gate = (d_activ * up * sigma * (1.0 + gate * (1.0 - sigma))).astype(bf16)
    d_up = (d_activ * silu).astype(bf16)
    d_gu = jnp.concatenate([d_gate, d_up], axis=1)
    d_xn2 = sum_tp(nt(d_gu, gu_l), nt(d_gu, gu_r))
    ffn_terms = sum_tp(nn(activ, down_l), nn(activ, down_r))
    layer = [(h + t.astype(f32)).astype(bf16) for h, t in zip(hidden, ffn_terms)]

    d_norm, ffn_gain_grad = norm_back(
        hidden, inverse_two, ffn_g, [d.astype(f32) for d in d_xn2], width
    )
    d_hidden = [a.astype(f32) + b for a, b in zip(dy, d_norm)]
    d_mixed = [a.astype(bf16) for a in d_hidden]
    d_attended = (nt(d_mixed[0], out_l) + nt(d_mixed[1], out_r)).astype(bf16)
    d_qlin, kv_own, kv_oth = attend_back(
        info, queries, attended, d_attended, log_totals, k_own, v_own, k_oth, v_oth, cosine, sine
    )
    kv_part = kv_own.astype(f32) + over_ctx(kv_oth).astype(f32)
    layer, d_qlin = lax.optimization_barrier((layer, d_qlin))
    layer_out = put_blocks(layer[0], layer[1], order)[None]
    d_qn, kv_grad = sum_tp(nt(d_qlin, query_up_full), kv_part)

    gu_grad = scatter(lambda: tn(xn2[0], d_gu), lambda: tn(xn2[1], d_gu), 0)
    down_grad = scatter(lambda: tn(activ, dy[0]), lambda: tn(activ, dy[1]), 1)
    out_grad = scatter(lambda: tn(attended, d_mixed[0]), lambda: tn(attended, d_mixed[1]), 1)
    qn_pair = take_blocks(qn, order)
    up_grad = scatter(lambda: tn(qn_pair[0], d_qlin), lambda: tn(qn_pair[1], d_qlin), 0)

    d_qn, kv_grad = d_qn.astype(f32), kv_grad.astype(f32)
    (d_latent,), (query_gain_grad,) = norm_back(
        [latent], inverse_latent, [query_g], [d_qn], rank
    )
    d_first = jnp.concatenate(
        [
            d_latent.astype(bf16),
            rotate(kv_grad[:, :head], cosine, -sine).astype(bf16),
            kv_grad[:, head:].astype(bf16),
        ],
        axis=1,
    )
    first_grad = scatter(lambda: tn(xn1[0], d_first), lambda: tn(xn1[1], d_first), 0)
    d_xn1 = [nt(d_first, first_l), nt(d_first, first_r)]
    d_x, attn_gain_grad = norm_back(x, inverse_one, attn_g, d_xn1, width)
    d_rows = [(a + b).astype(bf16) for a, b in zip(d_hidden, d_x)]
    tokens_grad = put_blocks(d_rows[0], d_rows[1], order)[None]

    query_gain_grad = query_gain_grad.reshape(8, -1)[order].reshape(2, -1)

    pieces = lax.axis_size("fsdp") * lax.axis_size("ctx") // 2

    def gain_part(k):
        parts = [attn_gain_grad[k], ffn_gain_grad[k], query_gain_grad[k]]
        row = jnp.concatenate([p.reshape(pieces, -1) for p in parts], axis=1).reshape(1, -1)
        return jnp.concatenate([row, row], axis=0)

    gain_grads = scatter(lambda: gain_part(0), lambda: gain_part(1), 1)[0]
    return (
        layer_out,
        tokens_grad,
        gain_grads[:n_gain],
        first_grad[:, :rank],
        gain_grads[2 * n_gain :],
        up_grad,
        first_grad[:, rank : rank + head],
        first_grad[:, rank + head :],
        out_grad,
        gain_grads[n_gain : 2 * n_gain],
        gu_grad[:, :units],
        gu_grad[:, units:],
        down_grad,
    )


def solution(mesh):
    return jax.shard_map(
        shards,
        mesh=mesh,
        in_specs=(
            P("fsdp", "ctx", None),
            P("fsdp", "ctx", None),
            P("fsdp", None),
            P(("fsdp", "ctx")),
            P(("fsdp", "ctx"), None),
            P(("fsdp", "ctx")),
            P(("fsdp", "ctx"), "tp"),
            P(("fsdp", "ctx"), None),
            P(("fsdp", "ctx"), None),
            P("tp", ("fsdp", "ctx")),
            P(("fsdp", "ctx")),
            P(("fsdp", "ctx"), "tp"),
            P(("fsdp", "ctx"), "tp"),
            P("tp", ("fsdp", "ctx")),
        ),
        out_specs=(
            P("fsdp", "ctx", None),
            P("fsdp", "ctx", None),
            P(("fsdp", "ctx")),
            P(("fsdp", "ctx"), None),
            P(("fsdp", "ctx")),
            P(("fsdp", "ctx"), "tp"),
            P(("fsdp", "ctx"), None),
            P(("fsdp", "ctx"), None),
            P("tp", ("fsdp", "ctx")),
            P(("fsdp", "ctx")),
            P(("fsdp", "ctx"), "tp"),
            P(("fsdp", "ctx"), "tp"),
            P("tp", ("fsdp", "ctx")),
        ),
        check_vma=False,
    )
```
